256 devices in a mesh: owner: 16 (over y, z_lo, core), dp: 16 (over z_hi, x).
Axes of the slice: x: 4, y: 4, z: 8 (z_hi: 4, z_lo: 2; z = z_hi * 2 + z_lo), core: 2. Of those that a mesh axis runs over, the one named last changes fastest.
Arguments:
- activations: bfloat16 [512, 8, 8, 512], P(('owner', 'dp')), may hold values from -8 to 8
- out_grad: bfloat16 [512, 8, 8, 512], P(('owner', 'dp')), may hold values from -6 to 6
- group_weight: bfloat16 [16, 288, 32], replicated, may hold values from -0.375 to 0.375
- proj_weight: bfloat16 [512, 512], replicated, may hold values from -0.25 to 0.25
- bn_gain: float32 [512], replicated, may hold values from 0.1 to 1.9
- bn_shift: float32 [512], replicated, may hold values from -3 to 3
- slot_block: int32 [16, 6], replicated, may hold values from -1 to 47, as said below
Outputs:
- group_grad: float32 [16, 288, 32], replicated
- proj_grad: float32 [512, 512], replicated
- out_factor: float32 [16, 32, 32], replicated
- factor_owned: float32 [96, 96, 288], P('owner', 'dp')
The draws below stay inside these ranges and needn't reach their ends.
Inputs may be any that keep to these rules, and one draw needn't show every extreme that they name: `slot_block`: each of the 48 blocks stands in exactly one slot; an owner's blocks fill its slots from the first, the rest hold -1; some owner's 6 slots are all used.
All inputs are finite; a program needn't handle non-finite values.
Results may differ from the reference program's by a relative error of at most 0.0065.
Values sent between devices are 32-bit elements; how exact they have to be, the bound alone decides.
A program may use at most 64 MiB of HBM per device.

```python
import math
import jax
import jax.numpy as jnp
from jax import lax

GRP = 16
GW = 32
COUT = 512
SIDE = 8
IMG_DEV = 2
CIN = 512
CPATCH = 288
BROWS = 96
NB = 48
SLOTS = 6
IMGS = 512
ROWS = 32768
N_OWNER = 16
N_DP = 16


def draw_activations(key, part):
    key_base, key_image, key_channel = jax.random.split(key, 3)
    shape = (IMGS, SIDE, SIDE, CIN)
    base = jax.random.normal(key_base, shape, jnp.float32)
    mixed = base + 0.7 * jnp.roll(base, 1, axis=3) + 0.5 * jnp.roll(base, 1, axis=2)
    image_scale = jnp.exp(0.7 * jax.random.uniform(key_image, (IMGS, 1, 1, 1), jnp.float32, -1.0, 1.0))
    channel_scale = jnp.exp(0.5 * jax.random.uniform(key_channel, (CIN,), jnp.float32, -1.0, 1.0))
    values = 0.6 * mixed * image_scale * channel_scale
    return jnp.clip(values, -8.0, 8.0).astype(jnp.bfloat16)


def draw_slot_block(key, part):
    key_order, key_busy = jax.random.split(key)
    block_order = jax.random.permutation(key_order, NB).astype(jnp.int32)
    busiest = jax.random.randint(key_busy, (), 0, N_OWNER)
    position = jnp.arange(NB, dtype=jnp.int32)
    beyond = jnp.maximum(position - SLOTS, 0)
    others = N_OWNER - 1
    owner_index = jnp.where(position < SLOTS, busiest, (busiest + 1 + beyond % others) % N_OWNER)
    slot_index = jnp.where(position < SLOTS, position, beyond // others)
    slot_table = jnp.full((N_OWNER, SLOTS), -1, jnp.int32)
    return slot_table.at[owner_index, slot_index].set(block_order)


def level_of(own_key, dims, shards, low, high):
    def one(axis_at, parts):
        draws = jax.random.uniform(jax.random.fold_in(jax.random.fold_in(own_key, 6), axis_at), (parts,), jnp.float32, low / len(shards), high / len(shards))
        return jnp.repeat(jnp.exp(draws), dims[axis_at] // parts).reshape((-1,) + (1,) * (len(dims) - axis_at - 1))

    loudness = one(*shards[0])
    for cut in shards[1:]:
        loudness = loudness * one(*cut)
    return loudness


def gaussian(key, shape, spread, reach, cuts=(), kind=jnp.bfloat16):
    array = jax.random.normal(key, shape, jnp.float32) * spread
    if len(cuts) > 0:
        array = level_of(key, shape, cuts, -0.22, 0.18) * array
    return jnp.clip(array, min=-reach, max=reach).astype(kind)


def setup_inputs(seed: int = 0) -> dict:
    keys = jax.random.split(jax.random.key(seed), 8)
    activations = draw_activations(jax.random.fold_in(keys[7], 71), 0)
    out_grad = gaussian(keys[1], (IMGS, SIDE, SIDE, COUT), 1.0, 6.0, ((0, 256),))
    group_weight = gaussian(keys[2], (GRP, CPATCH, GW), CPATCH ** -0.5, 0.375)
    proj_weight = gaussian(keys[3], (CIN, COUT), CIN ** -0.5, 0.25)
    bn_gain = jnp.clip(1.0 + 0.18 * jax.random.normal(keys[4], (CIN,), jnp.float32), 0.1, 1.9)
    bn_shift = gaussian(keys[5], (CIN,), 0.5, 3.0, (), jnp.float32)
    slot_block = draw_slot_block(jax.random.fold_in(keys[7], 71), 0)
    return dict(activations=activations, out_grad=out_grad, group_weight=group_weight, proj_weight=proj_weight, bn_gain=bn_gain, bn_shift=bn_shift, slot_block=slot_block)


def patch_rows(images):
    count = images.shape[0]
    padded = jnp.pad(images, ((0, 0), (1, 1), (1, 1), (0, 0)))
    padded = padded.reshape(count, SIDE + 2, SIDE + 2, GRP, GW)
    shifted = [padded[:, row_shift:row_shift + SIDE, col_shift:col_shift + SIDE] for row_shift in range(3) for col_shift in range(3)]
    return jnp.stack(shifted, axis=4).reshape(count * SIDE * SIDE, GRP, 9 * GW)

def reference(activations, out_grad, group_weight, proj_weight, bn_gain, bn_shift, slot_block):
    blocks_count = N_OWNER * N_DP
    act_blocks = activations.reshape(blocks_count, IMG_DEV, SIDE, SIDE, CIN)
    grad_blocks = out_grad.reshape(blocks_count, IMG_DEV * SIDE * SIDE, COUT)
    weight_full = group_weight.astype(jnp.float32)
    proj_full = proj_weight.astype(jnp.float32)

    def accumulate(carry, pieces):
        group_sum, proj_sum, out_sum, in_sum = carry
        images, upstream = pieces
        patches = patch_rows(images).astype(jnp.float32)
        conv_out = jnp.einsum('rgp,gpo->rgo', patches, weight_full).reshape(-1, CIN)
        preact = conv_out * bn_gain + bn_shift
        hidden = jnp.maximum(preact, 0.0).astype(jnp.bfloat16)
        upstream_full = upstream.astype(jnp.float32)
        back_grad = jnp.einsum('ro,co->rc', upstream_full, proj_full)
        grad_pre = jnp.where(preact > 0.0, back_grad * bn_gain, 0.0).astype(jnp.bfloat16)
        grad_pre = lax.optimization_barrier(grad_pre)
        grad_full = grad_pre.astype(jnp.float32).reshape(-1, GRP, GW)
        hidden_full = hidden.astype(jnp.float32)
        group_sum = group_sum + jnp.einsum('rgp,rgo->gpo', patches, grad_full)
        proj_sum = proj_sum + jnp.einsum('rc,ro->co', hidden_full, upstream_full)
        out_sum = out_sum + jnp.einsum('rga,rgb->gab', grad_full, grad_full)
        in_sum = in_sum + jnp.einsum('rgp,rgq->gpq', patches, patches)
        return ((group_sum, proj_sum, out_sum, in_sum), None)
    start = (jnp.zeros((GRP, CPATCH, GW), jnp.float32), jnp.zeros((CIN, COUT), jnp.float32), jnp.zeros((GRP, GW, GW), jnp.float32), jnp.zeros((GRP, CPATCH, CPATCH), jnp.float32))
    sums, _ = lax.scan(accumulate, start, (act_blocks, grad_blocks))
    group_sum, proj_sum, out_sum, in_sum = sums
    grad_scale = 1.0 / math.sqrt(ROWS)
    mean_scale = 1.0 / ROWS
    factor_blocks = in_sum.reshape(NB, BROWS, CPATCH)
    flat_slots = slot_block.reshape(-1)
    picked = jnp.take(factor_blocks, jnp.clip(flat_slots, 0, NB - 1), axis=0)
    live = (flat_slots >= 0).astype(jnp.float32)
    factor_owned = picked * live[:, None, None] * mean_scale
    return (group_sum * grad_scale, proj_sum * grad_scale, out_sum * mean_scale, factor_owned)
```

```python
import functools
import math

import jax
import jax.numpy as jnp
from jax import lax
from jax.experimental import pallas as pl
from jax.experimental.pallas import tpu as pltpu
from jax.sharding import PartitionSpec as P

MESH = pl.DeviceIdType.MESH
F32 = jnp.float32
BF16 = jnp.bfloat16
NT = (((1,), (1,)), ((), ()))
GROUPS, GW, CP = 16, 32, 288
N_OWNER, N_DP = 16, 16


def shifted_rows(tile, lane, store):
    row = (lane // 8) % 8
    col = lane % 8
    for a in range(3):
        for b in range(3):
            offset = (a - 1) * 8 + (b - 1)
            moved = tile if offset == 0 else pltpu.roll(tile, (-offset) % 128, 1)
            keep = None
            if a == 0:
                keep = row >= 1
            if a == 2:
                keep = row <= 6
            if b == 0:
                keep = (col >= 1) if keep is None else keep & (col >= 1)
            if b == 2:
                keep = (col <= 6) if keep is None else keep & (col <= 6)
            if keep is not None:
                moved = jnp.where(keep, moved, 0.0)
            store(3 * a + b, moved.astype(BF16))


def kernel(
    grad_scale, mean_scale,
    slot_ref, x_ref, u_ref, gw_ref, pw_ref, gain_ref, shift_ref,
    group_out, proj_out, outf_out, fact_out,
    x_t, g_t, rx, rg, pt, zt, gram, ppart, rcore, pacc, rpx, rpy, rpz,
    fg_send, rfg, zh_send, rzh, gfull, ffull,
    barrier_free,
    sx, rxs, sg, rgs, s_core, r_core, s_px, r_px, s_py, r_py, s_pz, r_pz,
    s_fg, r_fg, s_zh, r_zh,
    s_ga, r_ga, s_fa, r_fa, s_pa, r_pa,
):
    del barrier_free
    owner = lax.axis_index("owner")
    dp = lax.axis_index("dp")
    core = owner % 2
    zlo = (owner // 2) % 2
    y = owner // 4
    x = dp % 4
    zhi = dp // 4
    z = zhi * 2 + zlo

    def at_y(j):
        return (((y + j) % 4) * 4 + zlo * 2 + core, dp)

    def at_x(j):
        return (owner, zhi * 4 + (x + j) % 4)

    def at_z(j):
        there = (z + j) % 8
        return (y * 4 + (there % 2) * 2 + core, (there // 2) * 4 + x)

    def at_zhi(j):
        return (owner, ((zhi + j) % 4) * 4 + x)

    at_zlo = (y * 4 + (1 - zlo) * 2 + core, dp)
    at_core = (y * 4 + zlo * 2 + (1 - core), dp)

    def copy(src, dst, send, recv, device):
        return pltpu.make_async_remote_copy(
            src_ref=src, dst_ref=dst, send_sem=send, recv_sem=recv, device_id=device, device_id_type=MESH
        )

    barrier = pltpu.get_barrier_semaphore()
    for j in range(1, N_OWNER):
        pl.semaphore_signal(barrier, inc=1, device_id=((owner + j) % N_OWNER, dp), device_id_type=MESH)
    for j in range(1, 4):
        pl.semaphore_signal(barrier, inc=1, device_id=at_x(j), device_id_type=MESH)
    for j in range(1, 8):
        pl.semaphore_signal(barrier, inc=1, device_id=at_z(j), device_id_type=MESH)

    x_rows = x_ref[...].astype(F32).T
    x_t[...] = x_rows.reshape(GROUPS, GW, 128)
    pl.semaphore_wait(barrier, 25)

    def x_copy(j):
        there = (owner + j) % N_OWNER
        return copy(x_t.at[there], rx.at[owner], sx.at[j], rxs.at[owner], (there, dp))

    def g_copy(j):
        there = (owner + j) % N_OWNER
        return copy(g_t.at[there], rg.at[owner], sg.at[j], rgs.at[owner], (there, dp))

    def send_x(j, carry):
        x_copy(j).start()
        return carry

    lax.fori_loop(1, N_OWNER, send_x, 0)

    lane = lax.broadcasted_iota(jnp.int32, (GW, 128), 1)
    gain_col = jnp.broadcast_to(gain_ref[...], (128, 512)).T
    shift_col = jnp.broadcast_to(shift_ref[...], (128, 512)).T
    conv = []
    for g in range(GROUPS):
        def put(s, value, g=g):
            pt[g, s * GW:(s + 1) * GW, :] = value

        shifted_rows(x_rows[g * GW:(g + 1) * GW, :], lane, put)
        weight_t = gw_ref[g].astype(F32).T.astype(BF16)
        conv.append(jnp.dot(weight_t, pt[g], preferred_element_type=F32))
    preact = jnp.concatenate(conv, axis=0) * gain_col + shift_col
    upstream = u_ref[...]
    back = lax.dot_general(pw_ref[...], upstream, NT, preferred_element_type=F32)
    grad = jnp.where(preact > 0.0, back * gain_col, 0.0).astype(BF16).astype(F32)
    g_t[...] = grad.reshape(GROUPS, GW, 128)

    def send_g(j, carry):
        g_copy(j).start()
        return carry

    lax.fori_loop(1, N_OWNER, send_g, 0)

    hidden = jnp.maximum(preact, 0.0).astype(BF16)
    ppart[...] = jnp.dot(hidden, upstream, preferred_element_type=F32)
    far = pl.multiple_of((1 - core) * 256, 256)
    near = pl.multiple_of(core * 256, 256)
    core_copy = copy(ppart.at[pl.ds(far, 256)], rcore, s_core, r_core, at_core)
    core_copy.start()

    rx[owner] = x_t[owner]
    rg[owner] = g_t[owner]

    core_copy.wait_recv()
    pacc[...] = ppart[pl.ds(near, 256), :] + rcore[...]
    px_copies = []
    for j in range(1, 4):
        rows = pl.ds(pl.multiple_of(((x + j) % 4) * 64, 64), 64)
        px_copies.append(copy(pacc.at[rows], rpx.at[x], s_px.at[j], r_px.at[x], at_x(j)))
        px_copies[-1].start()

    def wait_in(ref, sems, slot, send):
        copy(ref, ref, send, sems.at[slot], at_core).wait_recv()

    zt[320:384, :] = jnp.zeros((64, 2048), BF16)
    for j in range(N_OWNER):
        source = (owner + j) % N_OWNER
        if j:
            wait_in(rx.at[source], rxs, source, sx.at[0])
        lanes = slice(j * 128, (j + 1) * 128)

        def put_z(s, value, lanes=lanes):
            zt[s * GW:(s + 1) * GW, lanes] = value

        shifted_rows(rx[source], lane, put_z)
    for j in range(N_OWNER):
        source = (owner + j) % N_OWNER
        if j:
            wait_in(rg.at[source], rgs, source, sg.at[0])
        zt[CP:CP + GW, j * 128:(j + 1) * 128] = rg[source].astype(BF16)
    gram[...] = lax.dot_general(zt[0:320, :], zt[...], NT, preferred_element_type=F32)

    for xx in range(4):
        for zz in range(4):
            for a in range(3):
                at = a * 96 + (zz * 4 + xx) * 6
                fg_send[xx, zz * 3 + a] = gram[at:at + 8, :]
        fg_send[xx, 12] = gram[CP + xx * 8:CP + xx * 8 + 8, :]
    fg_copies = []
    for j in range(1, 4):
        fg_copies.append(copy(fg_send.at[(x + j) % 4], rfg.at[x], s_fg.at[j], r_fg.at[x], at_x(j)))
        fg_copies[-1].start()

    own = pacc[pl.ds(pl.multiple_of(x * 64, 64), 64), :]
    for j in range(1, 4):
        slot = (x + j) % 4
        wait_in(rpx.at[slot], r_px, slot, s_px.at[0])
        own = own + rpx[slot]
    for copied in px_copies:
        copied.wait_send()
    pacc[0:64, :] = own
    py_copies = []
    for j in range(1, 4):
        rows = pl.ds(pl.multiple_of(((y + j) % 4) * 16, 16), 16)
        py_copies.append(copy(pacc.at[rows], rpy.at[y], s_py.at[j], r_py.at[y], at_y(j)))
        py_copies[-1].start()

    for j in range(1, 4):
        slot = (x + j) % 4
        wait_in(rfg.at[slot], r_fg, slot, s_fg.at[0])
    rfg[x] = fg_send[x]
    summed = (rfg[0] + rfg[1]) + (rfg[2] + rfg[3])
    for zz in range(4):
        zh_send[zz, 0:3] = summed[zz * 3:zz * 3 + 3]
        zh_send[zz, 3] = summed[12]
    zh_copies = []
    for j in range(1, 4):
        there = (zhi + j) % 4
        zh_copies.append(copy(zh_send.at[there], rzh.at[zhi], s_zh.at[j], r_zh.at[zhi], at_zhi(j)))
        zh_copies[-1].start()

    own = pacc[pl.ds(pl.multiple_of(y * 16, 16), 16), :]
    for j in range(1, 4):
        slot = (y + j) % 4
        wait_in(rpy.at[slot], r_py, slot, s_py.at[0])
        own = own + rpy[slot]
    for copied in py_copies:
        copied.wait_send()
    pacc[64:80, :] = own
    pz_copies = []

    def tile_of(there, base):
        return (
            pl.ds(pl.multiple_of(base + 8 * (there // 4), 8), 8),
            pl.ds(pl.multiple_of(128 * (there % 4), 128), 128),
        )

    for j in range(1, 8):
        there = (z + j) % 8
        pz_copies.append(copy(pacc.at[tile_of(there, 64)], rpz.at[z], s_pz.at[j], r_pz.at[z], at_z(j)))
        pz_copies[-1].start()

    for j in range(1, 4):
        slot = (zhi + j) % 4
        wait_in(rzh.at[slot], r_zh, slot, s_zh.at[0])
    rzh[zhi] = zh_send[zhi]
    summed = (rzh[0] + rzh[1]) + (rzh[2] + rzh[3])
    place = core * 8 + y * 2 + zlo
    ffull[place] = summed[0:3] * mean_scale
    wide = lax.broadcasted_iota(jnp.int32, (8, 384), 1)
    row8 = pl.ds(pl.multiple_of(x * 8, 8), 8)
    gfull[place, row8, :] = summed[3] * jnp.where(wide < CP, grad_scale, mean_scale)
    f_zlo = copy(ffull.at[place], ffull.at[place], s_fa.at[0], r_fa.at[0], at_zlo)
    f_zlo.start()
    gx_copies = []
    for j in range(1, 4):
        piece = gfull.at[place, row8]
        gx_copies.append(copy(piece, piece, s_ga.at[j], r_ga.at[x], at_x(j)))
        gx_copies[-1].start()

    own = pacc[tile_of(z, 64)]
    for j in range(1, 8):
        slot = (z + j) % 8
        wait_in(rpz.at[slot], r_pz, slot, s_pz.at[0])
        own = own + rpz[slot]
    base16 = core * 256 + x * 64 + y * 16
    tile = tile_of(z, base16)
    proj_out[tile] = own * grad_scale
    pa_z = []
    for j in range(1, 8):
        piece = proj_out.at[tile]
        pa_z.append(copy(piece, piece, s_pa.at[j], r_pa.at[z], at_z(j)))
        pa_z[-1].start()

    pair = pl.ds(pl.multiple_of(core * 8 + y * 2, 2), 2)
    other_place = core * 8 + y * 2 + (1 - zlo)
    wait_in(ffull.at[other_place], r_fa, 0, s_fa.at[0])
    f_y = []
    for j in range(1, 4):
        f_y.append(copy(ffull.at[pair], ffull.at[pair], s_fa.at[j], r_fa.at[1 + y], at_y(j)))
        f_y[-1].start()
    for j in range(1, 4):
        slot = (x + j) % 4
        wait_in(gfull.at[place, pl.ds(pl.multiple_of(slot * 8, 8), 8)], r_ga, slot, s_ga.at[0])
    g_zlo = copy(gfull.at[place], gfull.at[place], s_ga.at[4], r_ga.at[4], at_zlo)
    g_zlo.start()

    for j in range(1, 8):
        slot = (z + j) % 8
        wait_in(proj_out.at[tile_of(slot, base16)], r_pa, slot, s_pa.at[0])
    pa_y = []
    for j in range(1, 4):
        piece = proj_out.at[pl.ds(pl.multiple_of(base16, 16), 16)]
        pa_y.append(copy(piece, piece, s_pa.at[8 + j], r_pa.at[8 + y], at_y(j)))
        pa_y[-1].start()

    wait_in(gfull.at[other_place], r_ga, 4, s_ga.at[0])
    g_y = []
    for j in range(1, 4):
        g_y.append(copy(gfull.at[pair], gfull.at[pair], s_ga.at[5 + j], r_ga.at[5 + y], at_y(j)))
        g_y[-1].start()

    half8 = pl.ds(pl.multiple_of(core * 8, 8), 8)
    other8 = pl.ds(pl.multiple_of((1 - core) * 8, 8), 8)
    for j in range(1, 4):
        slot = (y + j) % 4
        wait_in(ffull.at[pl.ds(pl.multiple_of(core * 8 + slot * 2, 2), 2)], r_fa, 1 + slot, s_fa.at[0])
    f_core = copy(ffull.at[half8], ffull.at[half8], s_fa.at[5], r_fa.at[5], at_core)
    f_core.start()

    base64 = core * 256 + x * 64
    for j in range(1, 4):
        slot = (y + j) % 4
        piece = proj_out.at[pl.ds(pl.multiple_of(base64 + slot * 16, 16), 16)]
        wait_in(piece, r_pa, 8 + slot, s_pa.at[0])
    pa_x = []
    for j in range(1, 4):
        piece = proj_out.at[pl.ds(pl.multiple_of(base64, 64), 64)]
        pa_x.append(copy(piece, piece, s_pa.at[12 + j], r_pa.at[12 + x], at_x(j)))
        pa_x[-1].start()

    for j in range(1, 4):
        slot = (y + j) % 4
        wait_in(gfull.at[pl.ds(pl.multiple_of(core * 8 + slot * 2, 2), 2)], r_ga, 5 + slot, s_ga.at[0])
    g_core = copy(gfull.at[half8], gfull.at[half8], s_ga.at[9], r_ga.at[9], at_core)
    g_core.start()

    for j in range(1, 4):
        slot = (x + j) % 4
        piece = proj_out.at[pl.ds(pl.multiple_of(core * 256 + slot * 64, 64), 64)]
        wait_in(piece, r_pa, 12 + slot, s_pa.at[0])
    piece = proj_out.at[pl.ds(near, 256)]
    pa_core = copy(piece, piece, s_pa.at[16], r_pa.at[16], at_core)
    pa_core.start()

    wait_in(ffull.at[other8], r_fa, 5, s_fa.at[0])
    for s in range(6):
        block = slot_ref[owner, s]
        which = jnp.maximum(block, 0)
        group = which // 3
        rows = ffull[(group % 2) * 8 + group // 2, which % 3]
        live = jnp.where(block >= 0, 1.0, 0.0).astype(F32)
        fact_out[s] = (rows * live)[0:6, 0:CP]

    wait_in(gfull.at[other8], r_ga, 9, s_ga.at[0])
    for g in range(GROUPS):
        rows = gfull[(g % 2) * 8 + g // 2]
        group_out[g] = rows.T[0:CP, :]
        outf_out[g] = rows[:, CP:CP + GW]

    wait_in(proj_out.at[pl.ds(far, 256)], r_pa, 16, s_pa.at[0])

    def sent(j, carry):
        x_copy(j).wait_send()
        g_copy(j).wait_send()
        return carry

    lax.fori_loop(1, N_OWNER, sent, 0)
    core_copy.wait_send()
    for copied in fg_copies + zh_copies + pz_copies + gx_copies + pa_z + f_y + pa_y + g_y + pa_x:
        copied.wait_send()
    for copied in (f_zlo, g_zlo, f_core, g_core, pa_core):
        copied.wait_send()


def per_device(activations, out_grad, group_weight, proj_weight, bn_gain, bn_shift, slot_block):
    rows = activations.shape[0] * activations.shape[1] * activations.shape[2]
    total_rows = rows * N_OWNER * N_DP
    grad_scale = 1.0 / math.sqrt(total_rows)
    mean_scale = 1.0 / total_rows
    vmem = pl.BlockSpec(memory_space=pltpu.VMEM)
    dma = pltpu.SemaphoreType.DMA
    return pl.pallas_call(
        functools.partial(kernel, grad_scale, mean_scale),
        out_shape=(
            jax.ShapeDtypeStruct((GROUPS, CP, GW), F32),
            jax.ShapeDtypeStruct((512, 512), F32),
            jax.ShapeDtypeStruct((GROUPS, GW, GW), F32),
            jax.ShapeDtypeStruct((6, 6, CP), F32),
        ),
        in_specs=[pl.BlockSpec(memory_space=pltpu.SMEM)] + [vmem] * 6,
        out_specs=(vmem,) * 4,
        scratch_shapes=[
            pltpu.VMEM((GROUPS, GW, 128), F32),
            pltpu.VMEM((GROUPS, GW, 128), F32),
            pltpu.VMEM((GROUPS, GW, 128), F32),
            pltpu.VMEM((GROUPS, GW, 128), F32),
            pltpu.VMEM((GROUPS, CP, 128), BF16),
            pltpu.VMEM((384, 2048), BF16),
            pltpu.VMEM((320, 384), F32),
            pltpu.VMEM((512, 512), F32),
            pltpu.VMEM((256, 512), F32),
            pltpu.VMEM((256, 512), F32),
            pltpu.VMEM((4, 64, 512), F32),
            pltpu.VMEM((4, 16, 512), F32),
            pltpu.VMEM((8, 8, 128), F32),
            pltpu.VMEM((4, 13, 8, 384), F32),
            pltpu.VMEM((4, 13, 8, 384), F32),
            pltpu.VMEM((4, 4, 8, 384), F32),
            pltpu.VMEM((4, 4, 8, 384), F32),
            pltpu.VMEM((GROUPS, GW, 384), F32),
            pltpu.VMEM((GROUPS, 3, 8, 384), F32),
            pltpu.SemaphoreType.REGULAR,
            dma((16,)), dma((16,)), dma((16,)), dma((16,)),
            dma, dma,
            dma((4,)), dma((4,)), dma((4,)), dma((4,)), dma((8,)), dma((8,)),
            dma((4,)), dma((4,)), dma((4,)), dma((4,)),
            dma((10,)), dma((10,)), dma((6,)), dma((6,)), dma((17,)), dma((17,)),
        ],
        compiler_params=pltpu.CompilerParams(
            collective_id=0, has_side_effects=True, vmem_limit_bytes=48 * 1024 * 1024
        ),
    )(
        slot_block,
        activations.reshape(rows, 512),
        out_grad.reshape(rows, 512),
        group_weight,
        proj_weight,
        bn_gain.reshape(1, 512),
        bn_shift.reshape(1, 512),
    )


def solution(mesh):
    placed = (
        P(("owner", "dp"), None, None, None),
        P(("owner", "dp"), None, None, None),
        P(),
        P(),
        P(),
        P(),
        P(),
    )
    return jax.shard_map(
        per_device,
        mesh=mesh,
        in_specs=placed,
        out_specs=(P(), P(), P(), P("owner", "dp", None)),
        check_vma=False,
    )
```

```python
import functools
import math

import jax
import jax.numpy as jnp
from jax import lax
from jax.experimental import pallas as pl
from jax.experimental.pallas import tpu as pltpu
from jax.sharding import PartitionSpec as P

MESH = pl.DeviceIdType.MESH
F32 = jnp.float32
BF16 = jnp.bfloat16
NT = (((1,), (1,)), ((), ()))
GROUPS, GW, CP = 16, 32, 288
N_OWNER, N_DP = 16, 16
MAIN, REST, FACT = 256, 768, 896
LEFT, RIGHT = slice(0, 256), slice(256, 512)


def shifted_rows(tile, lane, store):
    row = (lane // 8) % 8
    col = lane % 8
    for a in range(3):
        for b in range(3):
            offset = (a - 1) * 8 + (b - 1)
            moved = tile if offset == 0 else pltpu.roll(tile, (-offset) % 128, 1)
            keep = None
            if a == 0:
                keep = row >= 1
            if a == 2:
                keep = row <= 6
            if b == 0:
                keep = (col >= 1) if keep is None else keep & (col >= 1)
            if b == 2:
                keep = (col <= 6) if keep is None else keep & (col <= 6)
            if keep is not None:
                moved = jnp.where(keep, moved, 0.0)
            store(3 * a + b, moved.astype(BF16))


def rows_at(start, size):
    return pl.ds(pl.multiple_of(start, size), size)


class Stage:
    def __init__(self, send, recv, base=0):
        self.send, self.recv, self.base = send, recv, base
        self.sent, self.due = [], []

    def put(self, src, dst, device, here, arrival, there):
        copy = pltpu.make_async_remote_copy(
            src_ref=src, dst_ref=dst, send_sem=self.send.at[self.base + len(self.sent)],
            recv_sem=self.recv.at[self.base + here], device_id=device, device_id_type=MESH,
        )
        copy.start()
        self.sent.append(copy)
        self.due.append(
            pltpu.make_async_remote_copy(
                src_ref=arrival, dst_ref=arrival, send_sem=self.send.at[self.base],
                recv_sem=self.recv.at[self.base + there], device_id=device, device_id_type=MESH,
            )
        )

    def take(self):
        self.due.pop(0).wait_recv()

    def take_all(self):
        while self.due:
            self.take()

    def drain(self):
        while self.sent:
            self.sent.pop(0).wait_send()


def kernel(
    grad_scale, mean_scale,
    x_hbm, u_hbm, gw_hbm, pw_hbm, gain_hbm, shift_hbm,
    gfull, pfull, ffull,
    x_in, u_in, gw_in, pw_in, gain_in, shift_in,
    x_t, g_t, rx, rg, pt, zt, gram, fcat, ppart, rcore, pacc, rp1, pmid, rp2, plast, rpl, rpz,
    f_send, rf, zh_send, rzh, gp_send, rgx, rgz,
    in_sem, sx, rxs, sg, rgs, s_p, r_p, s_f, r_f, s_g, r_g,
):
    loads = [
        pltpu.make_async_copy(src, dst, in_sem.at[i])
        for i, (src, dst) in enumerate(
            ((x_hbm, x_in), (u_hbm, u_in), (gw_hbm, gw_in), (pw_hbm, pw_in), (gain_hbm, gain_in), (shift_hbm, shift_in))
        )
    ]
    for load in loads:
        load.start()

    owner = lax.axis_index("owner")
    dp = lax.axis_index("dp")
    core = owner % 2
    zlo = (owner // 2) % 2
    y = owner // 4
    x = dp % 4
    zhi = dp // 4

    def at_y(j):
        return (((y + j) % 4) * 4 + zlo * 2 + core, dp)

    def at_x(j):
        return (owner, zhi * 4 + (x + j) % 4)

    def at_zhi(j):
        return (owner, ((zhi + j) % 4) * 4 + x)

    at_zlo = (y * 4 + (1 - zlo) * 2 + core, dp)
    at_core = (y * 4 + zlo * 2 + (1 - core), dp)

    barrier = pltpu.get_barrier_semaphore()
    for j in range(1, N_OWNER):
        pl.semaphore_signal(barrier, inc=1, device_id=((owner + j) % N_OWNER, dp), device_id_type=MESH)
    for j in range(1, 4):
        pl.semaphore_signal(barrier, inc=1, device_id=at_x(j), device_id_type=MESH)
        pl.semaphore_signal(barrier, inc=1, device_id=at_zhi(j), device_id_type=MESH)

    loads[0].wait()
    x_rows = x_in[...].astype(F32).T
    x_t[...] = x_rows.reshape(GROUPS, GW, 128)
    pl.semaphore_wait(barrier, 21)

    def exchange(own, landed, send, recv):
        stage = Stage(send, recv)
        for j in range(1, N_OWNER):
            there = (owner + j) % N_OWNER
            source = (owner + N_OWNER - j) % N_OWNER
            stage.put(own.at[there], landed.at[owner], (there, dp), owner, landed.at[source], source)
        return stage

    x_stage = exchange(x_t, rx, sx, rxs)
    stages = [x_stage]
    rx[owner] = x_t[owner]

    lane = lax.broadcasted_iota(jnp.int32, (GW, 128), 1)
    for load in loads[1:]:
        load.wait()
    gain_col = jnp.broadcast_to(gain_in[...], (128, 512)).T
    shift_col = jnp.broadcast_to(shift_in[...], (128, 512)).T
    upstream = u_in[...]
    back = lax.dot_general(pw_in[...], upstream, NT, preferred_element_type=F32)
    conv = []
    for g in range(GROUPS):
        def put(s, value, g=g):
            pt[g, s * GW:(s + 1) * GW, :] = value

        shifted_rows(x_rows[g * GW:(g + 1) * GW, :], lane, put)
        conv.append(jnp.dot(gw_in[g], pt[g], preferred_element_type=F32))
    preact = jnp.concatenate(conv, axis=0) * gain_col + shift_col
    grad = jnp.where(preact > 0.0, back * gain_col, 0.0).astype(BF16).astype(F32)
    g_t[...] = grad.reshape(GROUPS, GW, 128)
    g_stage = exchange(g_t, rg, sg, rgs)
    stages.append(g_stage)
    rg[owner] = g_t[owner]

    hidden = jnp.maximum(preact, 0.0).astype(BF16)
    ppart[...] = jnp.dot(hidden, upstream, preferred_element_type=F32)
    far, near = rows_at((1 - core) * 256, 256), rows_at(core * 256, 256)
    pc = Stage(s_p, r_p, 0)
    pc.put(ppart.at[far], rcore, at_core, 0, rcore, 0)
    stages.append(pc)

    pc.take()
    pacc[...] = ppart[near, :] + rcore[...]
    px, py = Stage(s_p, r_p, 1), Stage(s_p, r_p, 5)
    stages += [px, py]
    for j in range(1, 4):
        slot = (x + j) % 4
        px.put(pacc.at[rows_at(slot * 64, 64), LEFT], rp1.at[x, :, LEFT], at_x(j), x, rp1.at[slot, :, LEFT], slot)
        slot = (y + j) % 4
        py.put(pacc.at[rows_at(slot * 64, 64), RIGHT], rp1.at[y, :, RIGHT], at_y(j), y, rp1.at[slot, :, RIGHT], slot)

    zt[320:384, :] = jnp.zeros((64, 2048), BF16)
    zh_send[:, 6:8, :] = jnp.zeros((4, 2, FACT), F32)
    for j in range(N_OWNER):
        source = (owner + N_OWNER - j) % N_OWNER
        if j:
            x_stage.take()
        lanes = slice(j * 128, (j + 1) * 128)

        def put_z(s, value, lanes=lanes):
            zt[s * GW:(s + 1) * GW, lanes] = value

        shifted_rows(rx[source], lane, put_z)

    gram[...] = lax.dot_general(zt[0:CP, :], zt[0:CP, :], NT, preferred_element_type=F32)
    for a in range(3):
        fcat[:, a * MAIN:(a + 1) * MAIN] = gram[a * 96:a * 96 + 96, 0:MAIN]
        fcat[:, REST + a * 32:REST + a * 32 + 32] = gram[a * 96:a * 96 + 96, MAIN:CP]
    fcat[:, REST + 96:FACT] = jnp.zeros((96, 32), F32)
    for xx in range(4):
        for zz in range(4):
            at = (zz * 4 + xx) * 6
            f_send[xx, zz * 6:zz * 6 + 6, :] = fcat[at:at + 6, :]
    fx = Stage(s_f, r_f, 0)
    stages.append(fx)
    for j in range(1, 4):
        slot = (x + j) % 4
        fx.put(f_send.at[slot], rf.at[x], at_x(j), x, rf.at[slot], slot)

    for j in range(N_OWNER):
        source = (owner + N_OWNER - j) % N_OWNER
        if j:
            g_stage.take()
        zt[CP:CP + GW, j * 128:(j + 1) * 128] = rg[source].astype(BF16)
    part = lax.dot_general(zt[CP:CP + GW, :], zt[...], NT, preferred_element_type=F32)
    gp_send[...] = part.reshape(4, 8, 384)
    gpx = Stage(s_g, r_g, 0)
    stages.append(gpx)
    for j in range(1, 4):
        slot = (x + j) % 4
        gpx.put(gp_send.at[slot], rgx.at[x], at_x(j), x, rgx.at[slot], slot)

    left = pacc[rows_at(x * 64, 64), LEFT]
    right = pacc[rows_at(y * 64, 64), RIGHT]
    for j in range(1, 4):
        px.take()
        left = left + rp1[(x + j) % 4, :, LEFT]
        py.take()
        right = right + rp1[(y + j) % 4, :, RIGHT]
    pmid[:, LEFT] = left
    pmid[:, RIGHT] = right
    py2, px2 = Stage(s_p, r_p, 9), Stage(s_p, r_p, 13)
    stages += [py2, px2]
    for j in range(1, 4):
        slot = (y + j) % 4
        py2.put(pmid.at[rows_at(slot * 16, 16), LEFT], rp2.at[y, :, LEFT], at_y(j), y, rp2.at[slot, :, LEFT], slot)
        slot = (x + j) % 4
        px2.put(pmid.at[rows_at(slot * 16, 16), RIGHT], rp2.at[x, :, RIGHT], at_x(j), x, rp2.at[slot, :, RIGHT], slot)

    fx.take_all()
    rf[x] = f_send[x]
    summed = (rf[0] + rf[1]) + (rf[2] + rf[3])
    for zz in range(4):
        zh_send[zz, 0:6, :] = summed[zz * 6:zz * 6 + 6]
    fz = Stage(s_f, r_f, 4)
    stages.append(fz)
    for j in range(1, 4):
        slot = (zhi + j) % 4
        fz.put(zh_send.at[slot], rzh.at[zhi], at_zhi(j), zhi, rzh.at[slot], slot)
    gpx.take_all()
    rgx[x] = gp_send[x]
    rgz[zhi] = (rgx[0] + rgx[1]) + (rgx[2] + rgx[3])
    gpz = Stage(s_g, r_g, 4)
    stages.append(gpz)
    for j in range(1, 4):
        slot = (zhi + j) % 4
        gpz.put(rgz.at[zhi], rgz.at[zhi], at_zhi(j), zhi, rgz.at[slot], slot)

    left = pmid[rows_at(y * 16, 16), LEFT]
    right = pmid[rows_at(x * 16, 16), RIGHT]
    for j in range(1, 4):
        py2.take()
        left = left + rp2[(y + j) % 4, :, LEFT]
        px2.take()
        right = right + rp2[(x + j) % 4, :, RIGHT]
    plast[:, LEFT] = left
    plast[:, RIGHT] = right
    plo = Stage(s_p, r_p, 17)
    stages.append(plo)
    plo.put(plast.at[rows_at((1 - zlo) * 8, 8)], rpl, at_zlo, 0, rpl, 0)
    plo.take()
    rpz[zhi] = plast[rows_at(zlo * 8, 8), :] + rpl[...]
    pz = Stage(s_p, r_p, 18)
    stages.append(pz)
    for j in range(1, 4):
        slot = (zhi + j) % 4
        pz.put(rpz.at[zhi], rpz.at[zhi], at_zhi(j), zhi, rpz.at[slot], slot)

    fz.take_all()
    rzh[zhi] = zh_send[zhi]
    place = core * 8 + y * 2 + zlo
    other_place = core * 8 + y * 2 + (1 - zlo)
    pair = rows_at(core * 8 + y * 2, 2)
    half8, other8 = rows_at(core * 8, 8), rows_at((1 - core) * 8, 8)
    row8 = rows_at(x * 8, 8)
    ffull[place] = ((rzh[0] + rzh[1]) + (rzh[2] + rzh[3])) * mean_scale
    fl = Stage(s_f, r_f, 8)
    stages.append(fl)
    fl.put(ffull.at[place], ffull.at[place], at_zlo, 0, ffull.at[other_place], 0)
    gpz.take_all()
    wide = lax.broadcasted_iota(jnp.int32, (8, 384), 1)
    total = (rgz[0] + rgz[1]) + (rgz[2] + rgz[3])
    gfull[place, row8, :] = total * jnp.where(wide < CP, grad_scale, mean_scale)
    gl = Stage(s_g, r_g, 8)
    stages.append(gl)
    piece = gfull.at[place, row8]
    gl.put(piece, piece, at_zlo, 0, gfull.at[other_place, row8], 0)
    fl.take()
    fy = Stage(s_f, r_f, 9)
    stages.append(fy)
    for j in range(1, 4):
        slot = (y + j) % 4
        fy.put(ffull.at[pair], ffull.at[pair], at_y(j), y, ffull.at[rows_at(core * 8 + slot * 2, 2)], slot)
    gl.take()
    gy = Stage(s_g, r_g, 9)
    stages.append(gy)
    for j in range(1, 4):
        slot = (y + j) % 4
        piece = gfull.at[pair, row8]
        gy.put(piece, piece, at_y(j), y, gfull.at[rows_at(core * 8 + slot * 2, 2), row8], slot)

    pz.take_all()
    total = ((rpz[0] + rpz[1]) + (rpz[2] + rpz[3])) * grad_scale
    base_l = core * 256 + x * 64
    base_r = core * 256 + y * 64
    fin_l, fin_r = rows_at(base_l + y * 16 + zlo * 8, 8), rows_at(base_r + x * 16 + zlo * 8, 8)
    oth_l, oth_r = rows_at(base_l + y * 16 + (1 - zlo) * 8, 8), rows_at(base_r + x * 16 + (1 - zlo) * 8, 8)
    pfull[fin_l, LEFT] = total[:, LEFT]
    pfull[fin_r, RIGHT] = total[:, RIGHT]
    pal, par = Stage(s_p, r_p, 22), Stage(s_p, r_p, 23)
    stages += [pal, par]
    pal.put(pfull.at[fin_l, LEFT], pfull.at[fin_l, LEFT], at_zlo, 0, pfull.at[oth_l, LEFT], 0)
    par.put(pfull.at[fin_r, RIGHT], pfull.at[fin_r, RIGHT], at_zlo, 0, pfull.at[oth_r, RIGHT], 0)
    pal.take()
    par.take()
    pay, pax = Stage(s_p, r_p, 24), Stage(s_p, r_p, 28)
    stages += [pay, pax]
    for j in range(1, 4):
        slot = (y + j) % 4
        piece = pfull.at[rows_at(base_l + y * 16, 16), LEFT]
        pay.put(piece, piece, at_y(j), y, pfull.at[rows_at(base_l + slot * 16, 16), LEFT], slot)
        slot = (x + j) % 4
        piece = pfull.at[rows_at(base_r + x * 16, 16), RIGHT]
        pax.put(piece, piece, at_x(j), x, pfull.at[rows_at(base_r + slot * 16, 16), RIGHT], slot)

    gy.take_all()
    gx = Stage(s_g, r_g, 13)
    stages.append(gx)
    for j in range(1, 4):
        slot = (x + j) % 4
        piece = gfull.at[half8, row8]
        gx.put(piece, piece, at_x(j), x, gfull.at[half8, rows_at(slot * 8, 8)], slot)
    pay.take_all()
    pax2 = Stage(s_p, r_p, 32)
    stages.append(pax2)
    for j in range(1, 4):
        slot = (x + j) % 4
        piece = pfull.at[rows_at(base_l, 64), LEFT]
        pax2.put(piece, piece, at_x(j), x, pfull.at[rows_at(core * 256 + slot * 64, 64), LEFT], slot)
    pax.take_all()
    pay2 = Stage(s_p, r_p, 36)
    stages.append(pay2)
    for j in range(1, 4):
        slot = (y + j) % 4
        piece = pfull.at[rows_at(base_r, 64), RIGHT]
        pay2.put(piece, piece, at_y(j), y, pfull.at[rows_at(core * 256 + slot * 64, 64), RIGHT], slot)

    fy.take_all()
    fc, gc, pcl, pcr = Stage(s_f, r_f, 13), Stage(s_g, r_g, 17), Stage(s_p, r_p, 40), Stage(s_p, r_p, 41)
    stages += [fc, gc, pcl, pcr]
    fc.put(ffull.at[half8], ffull.at[half8], at_core, 0, ffull.at[other8], 0)
    gx.take_all()
    gc.put(gfull.at[half8], gfull.at[half8], at_core, 0, gfull.at[other8], 0)
    pay2.take_all()
    pcr.put(pfull.at[near, RIGHT], pfull.at[near, RIGHT], at_core, 0, pfull.at[far, RIGHT], 0)
    pax2.take_all()
    pcl.put(pfull.at[near, LEFT], pfull.at[near, LEFT], at_core, 0, pfull.at[far, LEFT], 0)
    for stage in stages:
        stage.take_all()
    for stage in stages:
        stage.drain()


def finish_kernel(slot_ref, gfull, pfull, ffull, group_out, proj_out, outf_out, fact_out, gs, os, fs, sem):
    owner = lax.axis_index("owner")
    copies = [pltpu.make_async_copy(pfull, proj_out, sem.at[0])]
    copies[0].start()
    for g in range(GROUPS):
        q = (g % 2) * 8 + g // 2
        gs[g] = gfull[q, :, 0:CP]
        os[g] = gfull[q, :, CP:CP + GW]
    copies.append(pltpu.make_async_copy(gs, group_out, sem.at[1]))
    copies.append(pltpu.make_async_copy(os, outf_out, sem.at[2]))
    copies[1].start()
    copies[2].start()
    for s in range(6):
        block = slot_ref[s, owner]
        which = jnp.maximum(block, 0)
        group, a = which // 3, which % 3
        rows = ffull[(group % 2) * 8 + group // 2]
        live = jnp.where(block >= 0, 1.0, 0.0).astype(F32)
        pick = [rows[:, k * MAIN:(k + 1) * MAIN] for k in range(3)]
        rest = [rows[:, REST + k * 32:REST + k * 32 + 32] for k in range(3)]
        for lanes, parts in ((slice(0, MAIN), pick), (slice(MAIN, CP), rest)):
            value = jnp.where(a == 0, parts[0], jnp.where(a == 1, parts[1], parts[2])) * live
            fs[s, :, lanes] = value[0:6]
    copies.append(pltpu.make_async_copy(fs, fact_out, sem.at[3]))
    copies[3].start()
    for copy in copies:
        copy.wait()


def per_device(activations, out_grad, group_weight, proj_weight, bn_gain, bn_shift, slot_block):
    rows = activations.shape[0] * activations.shape[1] * activations.shape[2]
    total_rows = rows * N_OWNER * N_DP
    grad_scale = 1.0 / math.sqrt(total_rows)
    mean_scale = 1.0 / total_rows
    vmem = pl.BlockSpec(memory_space=pltpu.VMEM)
    hbm = pl.BlockSpec(memory_space=pltpu.HBM)
    dma = pltpu.SemaphoreType.DMA
    full = pl.pallas_call(
        functools.partial(kernel, grad_scale, mean_scale),
        out_shape=(
            jax.ShapeDtypeStruct((GROUPS, GW, 384), F32),
            jax.ShapeDtypeStruct((512, 512), F32),
            jax.ShapeDtypeStruct((GROUPS, 8, FACT), F32),
        ),
        in_specs=[hbm] * 6,
        out_specs=(vmem,) * 3,
        scratch_shapes=[
            pltpu.VMEM((rows, 512), BF16),
            pltpu.VMEM((rows, 512), BF16),
            pltpu.VMEM((GROUPS, GW, CP), BF16),
            pltpu.VMEM((512, 512), BF16),
            pltpu.VMEM((1, 512), F32),
            pltpu.VMEM((1, 512), F32),
            pltpu.VMEM((GROUPS, GW, 128), F32),
            pltpu.VMEM((GROUPS, GW, 128), F32),
            pltpu.VMEM((GROUPS, GW, 128), F32),
            pltpu.VMEM((GROUPS, GW, 128), F32),
            pltpu.VMEM((GROUPS, CP, 128), BF16),
            pltpu.VMEM((384, 2048), BF16),
            pltpu.VMEM((CP, CP), F32),
            pltpu.VMEM((96, FACT), F32),
            pltpu.VMEM((512, 512), F32),
            pltpu.VMEM((256, 512), F32),
            pltpu.VMEM((256, 512), F32),
            pltpu.VMEM((4, 64, 512), F32),
            pltpu.VMEM((64, 512), F32),
            pltpu.VMEM((4, 16, 512), F32),
            pltpu.VMEM((16, 512), F32),
            pltpu.VMEM((8, 512), F32),
            pltpu.VMEM((4, 8, 512), F32),
            pltpu.VMEM((4, 24, FACT), F32),
            pltpu.VMEM((4, 24, FACT), F32),
            pltpu.VMEM((4, 8, FACT), F32),
            pltpu.VMEM((4, 8, FACT), F32),
            pltpu.VMEM((4, 8, 384), F32),
            pltpu.VMEM((4, 8, 384), F32),
            pltpu.VMEM((4, 8, 384), F32),
            dma((6,)),
            dma((16,)), dma((16,)), dma((16,)), dma((16,)),
            dma((42,)), dma((42,)), dma((14,)), dma((14,)), dma((18,)), dma((18,)),
        ],
        compiler_params=pltpu.CompilerParams(
            collective_id=0, has_side_effects=True
        ),
    )(
        activations.reshape(rows, 512),
        out_grad.reshape(rows, 512),
        jnp.swapaxes(group_weight, 1, 2),
        proj_weight,
        bn_gain.reshape(1, 512),
        bn_shift.reshape(1, 512),
    )
    group_grad, proj_grad, out_factor, owned = pl.pallas_call(
        finish_kernel,
        out_shape=(
            jax.ShapeDtypeStruct((GROUPS, GW, CP), F32),
            jax.ShapeDtypeStruct((512, 512), F32),
            jax.ShapeDtypeStruct((GROUPS, GW, GW), F32),
            jax.ShapeDtypeStruct((6, 6, CP), F32),
        ),
        in_specs=[pl.BlockSpec(memory_space=pltpu.SMEM)] + [vmem] * 3,
        out_specs=(hbm,) * 4,
        scratch_shapes=[
            pltpu.VMEM((GROUPS, GW, CP), F32),
            pltpu.VMEM((GROUPS, GW, GW), F32),
            pltpu.VMEM((6, 6, CP), F32),
            dma((4,)),
        ],
    )(slot_block.T, *full)
    return jnp.swapaxes(group_grad, 1, 2), proj_grad, out_factor, owned


def solution(mesh):
    placed = (
        P(("owner", "dp"), None, None, None),
        P(("owner", "dp"), None, None, None),
        P(),
        P(),
        P(),
        P(),
        P(),
    )
    return jax.shard_map(
        per_device,
        mesh=mesh,
        in_specs=placed,
        out_specs=(P(), P(), P(), P("owner", "dp", None)),
        check_vma=False,
    )
```
